32 devices in a mesh: dp: 8 (over z, core), mp: 4 (over y, x).
Axes of the slice: x: 2, y: 2, z: 4, core: 2. Of those that a mesh axis runs over, the one named last changes fastest.
Arguments:
- momentum: float32 [8, 256, 5120], P('dp', 'mp'), may hold values from -60 to 60
- gradient: bfloat16 [8, 256, 5120], P('dp', 'mp'), may hold values from -60 to 60
- columns: int32 [256], replicated, may hold values from 0 to 5119, as said below
Outputs:
- update: bfloat16 [256, 5120], P('mp', 'dp')
- new_momentum: float32 [8, 256, 5120], P('dp', 'mp')
The draws below stay inside these ranges and needn't reach their ends.
Inputs may be any that keep to these rules, and one draw needn't show every extreme that they name: `columns`: 256 distinct frequencies, 0 and 5119 always among them, in no particular order.
All inputs are finite; a program needn't handle non-finite values.
Results may differ from the reference program's by a relative error of at most 0.007.
Values may be sent and summed in bfloat16 or wider, within the bound.
A program may use at most 64 MiB of HBM per device.

```python
import math
import jax
import jax.numpy as jnp
from jax import lax

COLS = 5120
RANK = 256
ITERS = 5
ROWS = 256
REPLICAS = 8


def field_scales(scale_key):
    first_key, second_key = jax.random.split(scale_key)
    row_scales = jnp.exp(jax.random.uniform(first_key, (ROWS,), jnp.float32, math.log(0.3), math.log(3.0)))
    row_scales = row_scales * (0.5 + jnp.arange(ROWS, dtype=jnp.float32) / ROWS)
    col_scales = jnp.exp(jax.random.uniform(second_key, (COLS,), jnp.float32, math.log(0.3), math.log(3.0)))
    return (row_scales, col_scales)


def draw_momentum(key, part):
    folded = jax.random.fold_in(key, 11)
    keys_list = jax.random.split(folded, 2)
    row_scales, col_scales = field_scales(keys_list[0])
    noise = jnp.clip(jax.random.normal(keys_list[1], (REPLICAS, ROWS, COLS), jnp.float32), -5.0, 5.0)
    return 0.5 * noise * row_scales[None, :, None] * col_scales[None, None, :]


def draw_gradient(key, part):
    folded = jax.random.fold_in(key, 23)
    keys_list = jax.random.split(folded, 3)
    row_scales, col_scales = field_scales(keys_list[0])
    own = jnp.clip(jax.random.normal(keys_list[1], (REPLICAS, ROWS, COLS), jnp.float32), -5.0, 5.0)
    shared = jnp.clip(jax.random.normal(keys_list[2], (ROWS, COLS), jnp.float32), -5.0, 5.0)
    noise = 0.6 * own + 0.8 * shared[None]
    return (noise * row_scales[None, :, None] * col_scales[None, None, :]).astype(jnp.bfloat16)


def draw_columns(key, part):
    folded = jax.random.fold_in(key, 37)
    first_key, second_key = jax.random.split(folded)
    inner = jax.random.permutation(first_key, COLS - 2)[:RANK - 2].astype(jnp.int32) + 1
    picked = jnp.concatenate([jnp.array([0, COLS - 1], dtype=jnp.int32), inner])
    order = jax.random.permutation(second_key, RANK)
    return picked[order]


def setup_inputs(seed: int = 0) -> dict:
    seeds = jax.random.split(jax.random.key(seed), 4)
    momentum = draw_momentum(jax.random.fold_in(seeds[3], 71), 0)
    gradient = draw_gradient(jax.random.fold_in(seeds[3], 71), 0)
    columns = draw_columns(jax.random.fold_in(seeds[3], 71), 0)
    return {"momentum": momentum, "gradient": gradient, "columns": columns}


inertia = 0.9
linear_term = 3.4445
cubic_term = -4.775
quintic_term = 2.0315

def dct_table(columns):
    positions = jnp.arange(COLS, dtype=jnp.int32)
    phase_index = (2 * positions[:, None] + 1) * columns[None, :].astype(jnp.int32) % (4 * COLS)
    angles = phase_index.astype(jnp.float32) * (math.pi / (2 * COLS))
    column_scale = jnp.where(columns == 0, math.sqrt(1.0 / COLS), math.sqrt(2.0 / COLS))
    return (jnp.cos(angles) * column_scale[None, :]).astype(jnp.bfloat16)

def orthogonalize(gram_matrix):
    squared_norm = jnp.trace(gram_matrix) + 1e-06
    inverse_norm = 1.0 / jnp.sqrt(squared_norm)
    identity = jnp.eye(gram_matrix.shape[0], dtype=gram_matrix.dtype)
    gram_now = gram_matrix * (inverse_norm * inverse_norm)
    mixing = identity * inverse_norm
    highest = lax.Precision.HIGHEST
    for _ in range(ITERS):
        polynomial = linear_term * identity + cubic_term * gram_now + quintic_term * jnp.dot(gram_now, gram_now, precision=highest)
        mixing = jnp.dot(mixing, polynomial, precision=highest)
        gram_now = jnp.dot(jnp.dot(polynomial, gram_now, precision=highest), polynomial, precision=highest)
    return mixing

def reference(momentum, gradient, columns):
    cosines = dct_table(columns)

    def encode(replica_pair):
        current = inertia * replica_pair[0] + replica_pair[1].astype(jnp.float32)
        return jnp.dot(current.astype(jnp.bfloat16), cosines, preferred_element_type=jnp.float32)
    encoded = lax.map(encode, (momentum, gradient))
    averaged = lax.optimization_barrier(jnp.sum(encoded, axis=0)) / REPLICAS
    gram_matrix = jnp.dot(averaged.T, averaged, precision=lax.Precision.HIGHEST)
    mixing = orthogonalize(gram_matrix)
    orthogonal = jnp.dot(averaged, mixing, precision=lax.Precision.HIGHEST).astype(jnp.bfloat16)
    coded_rows = averaged.astype(jnp.bfloat16)
    direction = jnp.dot(orthogonal, cosines.T, preferred_element_type=jnp.float32)
    update = (direction * math.sqrt(ROWS * COLS / RANK)).astype(jnp.bfloat16)
    decoded = jnp.dot(coded_rows, cosines.T, preferred_element_type=jnp.float32)

    def refresh(replica_pair):
        current = inertia * replica_pair[0] + replica_pair[1].astype(jnp.float32)
        return current - decoded
    new_momentum = lax.map(refresh, (momentum, gradient))
    return (update, new_momentum)
```

```python
import functools
import math

import jax
import jax.numpy as jnp
from jax import lax
from jax.experimental import pallas as pl
from jax.experimental.pallas import tpu as pltpu
from jax.sharding import PartitionSpec as P

ITERS = 5
BLOCK = 64
CHUNK_BLOCKS = 8

inertia = 0.9
linear_term = 3.4445
cubic_term = -4.775
quintic_term = 2.0315
MESH = pl.DeviceIdType.MESH


def cos_sin(index, period):
    quarter = period // 4
    turns = jnp.floor(index * (1.0 / quarter) + 0.5)
    angle = (index - turns * quarter) * (2.0 * math.pi / period)
    quadrant = turns - 4.0 * jnp.floor(turns * 0.25)
    x2 = angle * angle
    sine = angle * (
        1.0 + x2 * (-1.0 / 6 + x2 * (1.0 / 120 + x2 * (-1.0 / 5040 + x2 * (1.0 / 362880))))
    )
    cosine = 1.0 + x2 * (
        -0.5 + x2 * (1.0 / 24 + x2 * (-1.0 / 720 + x2 * (1.0 / 40320 - x2 * (1.0 / 3628800))))
    )
    odd = (quadrant == 1.0) | (quadrant == 3.0)
    cos_part = jnp.where(odd, sine, cosine)
    sin_part = jnp.where(odd, cosine, sine)
    cos_out = jnp.where((quadrant == 1.0) | (quadrant == 2.0), -cos_part, cos_part)
    sin_out = jnp.where(quadrant >= 2.0, -sin_part, sin_part)
    return cos_out, sin_out


def split(x):
    high = x.astype(jnp.bfloat16)
    return high, (x - high.astype(jnp.float32)).astype(jnp.bfloat16)


def dot(a, b, dims=((1,), (0,))):
    return lax.dot_general(a, b, (dims, ((), ())), preferred_element_type=jnp.float32)


def dot3(a, b, dims=((1,), (0,))):
    return dot(a[0], b[0], dims) + dot(a[0], b[1], dims) + dot(a[1], b[0], dims)


def kernel(
    replicas,
    blocks,
    momentum_hbm,
    gradient_hbm,
    columns_ref,
    update_ref,
    new_hbm,
    current,
    grad,
    basis,
    cos_high,
    sin_high,
    out,
    encoded,
    swap_in,
    parts,
    full,
    load_sems,
    store_sems,
    swap_sems,
    z_send,
    z_recv,
    m_send,
    m_recv,
    f_send,
    f_recv,
):
    rows, cols = current.shape
    rank = basis.shape[1]
    half = rows // 2
    pairs = replicas // 2
    chunk = BLOCK * CHUNK_BLOCKS
    chunks = cols // chunk
    me_dp = lax.axis_index("dp")
    me_mp = lax.axis_index("mp")
    core = lax.rem(me_dp, 2)
    me_z = lax.div(me_dp, 2)
    partner = me_dp + 1 - 2 * core

    def load(step):
        span = pl.ds(pl.multiple_of(step * chunk, chunk), chunk)
        return (
            pltpu.make_async_copy(
                momentum_hbm.at[0, :, span], current.at[:, span], load_sems.at[0, step]
            ),
            pltpu.make_async_copy(
                gradient_hbm.at[0, :, span], grad.at[:, span], load_sems.at[1, step]
            ),
        )

    for step in range(chunks):
        for copy in load(step):
            copy.start()

    def z_peer(offset):
        return lax.rem(me_z + offset, pairs)

    def m_peer(offset):
        return lax.rem(me_mp + offset, blocks)

    barrier = pltpu.get_barrier_semaphore()
    pl.semaphore_signal(
        barrier, inc=1, device_id={"dp": partner, "mp": me_mp}, device_id_type=MESH
    )
    for offset in range(1, pairs):
        pl.semaphore_signal(
            barrier,
            inc=1,
            device_id={"dp": 2 * z_peer(offset) + core, "mp": me_mp},
            device_id_type=MESH,
        )
    for offset in range(1, blocks):
        pl.semaphore_signal(
            barrier,
            inc=1,
            device_id={"dp": me_dp, "mp": m_peer(offset)},
            device_id_type=MESH,
        )

    frequency = columns_ref[...].astype(jnp.float32)
    scale = jnp.where(columns_ref[...] == 0, math.sqrt(1.0 / cols), math.sqrt(2.0 / cols))
    high_count = cos_high.shape[0]
    high_index = lax.broadcasted_iota(jnp.int32, (high_count, rank), 0).astype(jnp.float32)
    ch, sh = cos_sin(high_index * frequency, 2 * cols // BLOCK)
    cos_high[...] = ch
    sin_high[...] = sh
    low_index = lax.broadcasted_iota(jnp.int32, (BLOCK, rank), 0).astype(jnp.float32)
    cl, sl = cos_sin((2.0 * low_index + 1.0) * frequency, 4 * cols)
    cl = cl * scale
    sl = sl * scale

    encoded[...] = jnp.zeros_like(encoded)

    def encode(step, carry):
        for block in range(CHUNK_BLOCKS):
            index = step * CHUNK_BLOCKS + block
            table = cos_high[pl.ds(index, 1), :] * cl - sin_high[pl.ds(index, 1), :] * sl
            start = pl.multiple_of(index * BLOCK, BLOCK)
            basis[pl.ds(start, BLOCK), :] = table.astype(jnp.bfloat16)
        for copy in load(step):
            copy.wait()
        span = pl.ds(pl.multiple_of(step * chunk, chunk), chunk)
        now = inertia * current[:, span] + grad[:, span].astype(jnp.float32)
        current[:, span] = now
        encoded[...] += dot(now.astype(jnp.bfloat16), basis[span, :])
        return carry

    lax.fori_loop(0, chunks, encode, 0)

    pl.semaphore_wait(barrier, 1 + (pairs - 1) + (blocks - 1))

    mine = pl.ds(pl.multiple_of(core * half, half), half)
    theirs = pl.ds(pl.multiple_of((1 - core) * half, half), half)
    swap = pltpu.make_async_remote_copy(
        src_ref=encoded.at[theirs, :],
        dst_ref=swap_in,
        send_sem=swap_sems.at[0],
        recv_sem=swap_sems.at[1],
        device_id={"dp": partner, "mp": me_mp},
        device_id_type=MESH,
    )
    swap.start()
    swap.wait()
    parts[me_z] = encoded[mine, :] + swap_in[...]

    z_copies = []
    for offset in range(1, pairs):
        copy = pltpu.make_async_remote_copy(
            src_ref=parts.at[me_z],
            dst_ref=parts.at[me_z],
            send_sem=z_send.at[offset],
            recv_sem=z_recv.at[offset],
            device_id={"dp": 2 * z_peer(offset) + core, "mp": me_mp},
            device_id_type=MESH,
        )
        copy.start()
        z_copies.append(copy)
    for copy in z_copies:
        copy.wait()
    total = parts[0]
    for index in range(1, pairs):
        total = total + parts[index]
    full[me_mp, core] = total * (1.0 / replicas)

    def forward(index):
        return pltpu.make_async_remote_copy(
            src_ref=full.at[index, core],
            dst_ref=full.at[index, core],
            send_sem=f_send.at[index],
            recv_sem=f_recv.at[index],
            device_id={"dp": partner, "mp": me_mp},
            device_id_type=MESH,
        )

    m_copies = []
    for offset in range(1, blocks):
        copy = pltpu.make_async_remote_copy(
            src_ref=full.at[me_mp, core],
            dst_ref=full.at[me_mp, core],
            send_sem=m_send.at[offset],
            recv_sem=m_recv.at[offset],
            device_id={"dp": me_dp, "mp": m_peer(offset)},
            device_id_type=MESH,
        )
        copy.start()
        m_copies.append(copy)
    own = forward(me_mp)
    own.start()
    own.wait()

    own_rows = full[me_mp].reshape(rows, rank)
    coded = own_rows.astype(jnp.bfloat16)

    def store(step):
        span = pl.ds(pl.multiple_of(step * chunk, chunk), chunk)
        return pltpu.make_async_copy(
            out.at[:, span], new_hbm.at[0, :, span], store_sems.at[step]
        )

    def refresh(step, carry):
        span = pl.ds(pl.multiple_of(step * chunk, chunk), chunk)
        out[:, span] = current[:, span] - dot(coded, basis[span, :], ((1,), (1,)))
        store(step).start()
        return carry

    lax.fori_loop(0, chunks, refresh, 0)

    passed = []
    for offset in range(1, blocks):
        m_copies[offset - 1].wait()
        copy = forward(lax.rem(me_mp + blocks - offset, blocks))
        copy.start()
        passed.append(copy)
    for copy in passed:
        copy.wait()

    averaged = full[...].reshape(blocks * rows, rank)
    pair = split(averaged)
    gram = dot3(pair, pair, ((0,), (0,)))
    inverse = lax.rsqrt(jnp.full((1, 1), 1e-06, jnp.float32) + jnp.sum(averaged * averaged))
    g = gram * (inverse * inverse)
    x = own_rows * inverse
    row = lax.broadcasted_iota(jnp.int32, (rank, rank), 0)
    col = lax.broadcasted_iota(jnp.int32, (rank, rank), 1)
    diagonal = jnp.where(row == col, linear_term, 0.0)
    for index in range(ITERS):
        g_pair = split(g)
        p = diagonal + cubic_term * g + quintic_term * dot3(g_pair, g_pair)
        p_pair = split(p)
        x = dot3(split(x), p_pair)
        if index < ITERS - 1:
            g = dot3(p_pair, split(dot3(p_pair, g_pair)))

    band = cols // replicas
    band_basis = basis[pl.ds(pl.multiple_of(me_dp * band, 16), band), :]
    direction = dot(x.astype(jnp.bfloat16), band_basis, ((1,), (1,)))
    update_scale = math.sqrt(rows * blocks * cols / rank)
    update_ref[...] = (direction * update_scale).astype(jnp.bfloat16)

    def drain(step, carry):
        store(step).wait()
        return carry

    lax.fori_loop(0, chunks, drain, 0)


def solution(mesh):
    replicas, blocks = mesh.shape["dp"], mesh.shape["mp"]

    def body(momentum, gradient, columns):
        _, rows, cols = momentum.shape
        rank = columns.shape[0]
        chunks = cols // (BLOCK * CHUNK_BLOCKS)
        pairs = replicas // 2
        dma = pltpu.SemaphoreType.DMA
        any_space = pl.BlockSpec(memory_space=pl.ANY)
        vmem_space = pl.BlockSpec(memory_space=pltpu.VMEM)
        return pl.pallas_call(
            functools.partial(kernel, replicas, blocks),
            out_shape=(
                jax.ShapeDtypeStruct((rows, cols // replicas), jnp.bfloat16),
                jax.ShapeDtypeStruct((1, rows, cols), jnp.float32),
            ),
            in_specs=[any_space, any_space, vmem_space],
            out_specs=(vmem_space, any_space),
            scratch_shapes=[
                pltpu.VMEM((rows, cols), jnp.float32),
                pltpu.VMEM((rows, cols), jnp.bfloat16),
                pltpu.VMEM((cols, rank), jnp.bfloat16),
                pltpu.VMEM((cols // BLOCK, rank), jnp.float32),
                pltpu.VMEM((cols // BLOCK, rank), jnp.float32),
                pltpu.VMEM((rows, cols), jnp.float32),
                pltpu.VMEM((rows, rank), jnp.float32),
                pltpu.VMEM((rows // 2, rank), jnp.float32),
                pltpu.VMEM((pairs, rows // 2, rank), jnp.float32),
                pltpu.VMEM((blocks, 2, rows // 2, rank), jnp.float32),
                dma((2, chunks)),
                dma((chunks,)),
                dma((2,)),
                dma((pairs,)),
                dma((pairs,)),
                dma((blocks,)),
                dma((blocks,)),
                dma((blocks,)),
                dma((blocks,)),
            ],
            compiler_params=pltpu.CompilerParams(collective_id=0, has_side_effects=True),
        )(momentum, gradient, columns.reshape(1, rank))

    return jax.shard_map(
        body,
        mesh=mesh,
        in_specs=(P("dp", "mp", None), P("dp", "mp", None), P()),
        out_specs=(P("mp", "dp"), P("dp", "mp", None)),
        check_vma=False,
    )
```

```python
import functools
import math

import jax
import jax.numpy as jnp
from jax import lax
from jax.experimental import pallas as pl
from jax.experimental.pallas import tpu as pltpu
from jax.sharding import PartitionSpec as P

ITERS = 5
BLOCK = 64
CHUNK_BLOCKS = 8

inertia = 0.9
linear_term = 3.4445
cubic_term = -4.775
quintic_term = 2.0315
VMEM_BYTES = 24 * 2**20
MESH = pl.DeviceIdType.MESH


def cos_sin(index, period):
    quarter = period // 4
    turns = jnp.floor(index * (1.0 / quarter) + 0.5)
    angle = (index - turns * quarter) * (2.0 * math.pi / period)
    quadrant = turns - 4.0 * jnp.floor(turns * 0.25)
    x2 = angle * angle
    sine = angle * (
        1.0 + x2 * (-1.0 / 6 + x2 * (1.0 / 120 + x2 * (-1.0 / 5040 + x2 * (1.0 / 362880))))
    )
    cosine = 1.0 + x2 * (
        -0.5 + x2 * (1.0 / 24 + x2 * (-1.0 / 720 + x2 * (1.0 / 40320 - x2 * (1.0 / 3628800))))
    )
    odd = (quadrant == 1.0) | (quadrant == 3.0)
    cos_part = jnp.where(odd, sine, cosine)
    sin_part = jnp.where(odd, cosine, sine)
    cos_out = jnp.where((quadrant == 1.0) | (quadrant == 2.0), -cos_part, cos_part)
    sin_out = jnp.where(quadrant >= 2.0, -sin_part, sin_part)
    return cos_out, sin_out


def split(x):
    high = x.astype(jnp.bfloat16)
    return high, (x - high.astype(jnp.float32)).astype(jnp.bfloat16)


def dot(a, b, dims=((1,), (0,))):
    return lax.dot_general(a, b, (dims, ((), ())), preferred_element_type=jnp.float32)


def dot3(a, b, dims=((1,), (0,))):
    return dot(a[0], b[0], dims) + dot(a[0], b[1], dims) + dot(a[1], b[0], dims)


def kernel(
    replicas,
    blocks,
    momentum_hbm,
    gradient_hbm,
    columns_ref,
    full_out,
    current,
    basis,
    grad,
    cos_high,
    sin_high,
    encoded,
    swap_in,
    parts,
    full,
    load_sems,
    swap_sems,
    z_send,
    z_recv,
    m_send,
    m_recv,
    f_send,
    f_recv,
):
    rows, cols = current.shape
    rank = basis.shape[1]
    half = rows // 2
    pairs = replicas // 2
    chunk = BLOCK * CHUNK_BLOCKS
    chunks = cols // chunk
    me_dp = lax.axis_index("dp")
    me_mp = lax.axis_index("mp")
    core = lax.rem(me_dp, 2)
    me_z = lax.div(me_dp, 2)
    partner = me_dp + 1 - 2 * core

    def load(step):
        span = pl.ds(pl.multiple_of(step * chunk, chunk), chunk)
        return (
            pltpu.make_async_copy(
                momentum_hbm.at[0, :, span], current.at[:, span], load_sems.at[0, step]
            ),
            pltpu.make_async_copy(
                gradient_hbm.at[0, :, span], grad.at[:, span], load_sems.at[1, step]
            ),
        )

    for step in range(chunks):
        for copy in load(step):
            copy.start()

    def z_peer(offset):
        return lax.rem(me_z + offset, pairs)

    def m_peer(offset):
        return lax.rem(me_mp + offset, blocks)

    barrier = pltpu.get_barrier_semaphore()
    pl.semaphore_signal(
        barrier, inc=1, device_id={"dp": partner, "mp": me_mp}, device_id_type=MESH
    )
    for offset in range(1, pairs):
        pl.semaphore_signal(
            barrier,
            inc=1,
            device_id={"dp": 2 * z_peer(offset) + core, "mp": me_mp},
            device_id_type=MESH,
        )
    for offset in range(1, blocks):
        pl.semaphore_signal(
            barrier,
            inc=1,
            device_id={"dp": me_dp, "mp": m_peer(offset)},
            device_id_type=MESH,
        )

    frequency = columns_ref[...].astype(jnp.float32)
    scale = jnp.where(columns_ref[...] == 0, math.sqrt(1.0 / cols), math.sqrt(2.0 / cols))
    high_count = cos_high.shape[0]
    high_index = lax.broadcasted_iota(jnp.int32, (high_count, rank), 0).astype(jnp.float32)
    ch, sh = cos_sin(high_index * frequency, 2 * cols // BLOCK)
    cos_high[...] = ch
    sin_high[...] = sh
    low_index = lax.broadcasted_iota(jnp.int32, (BLOCK, rank), 0).astype(jnp.float32)
    cl, sl = cos_sin((2.0 * low_index + 1.0) * frequency, 4 * cols)
    cl = cl * scale
    sl = sl * scale

    encoded[...] = jnp.zeros_like(encoded)

    def encode(step, carry):
        for block in range(CHUNK_BLOCKS):
            index = step * CHUNK_BLOCKS + block
            table = cos_high[pl.ds(index, 1), :] * cl - sin_high[pl.ds(index, 1), :] * sl
            start = pl.multiple_of(index * BLOCK, BLOCK)
            basis[pl.ds(start, BLOCK), :] = table.astype(jnp.bfloat16)
        for copy in load(step):
            copy.wait()
        span = pl.ds(pl.multiple_of(step * chunk, chunk), chunk)
        now = inertia * current[:, span] + grad[:, span].astype(jnp.float32)
        current[:, span] = now
        encoded[...] += dot(now.astype(jnp.bfloat16), basis[span, :])
        return carry

    lax.fori_loop(0, chunks, encode, 0)

    pl.semaphore_wait(barrier, 1 + (pairs - 1) + (blocks - 1))

    mine = pl.ds(pl.multiple_of(core * half, half), half)
    theirs = pl.ds(pl.multiple_of((1 - core) * half, half), half)
    swap = pltpu.make_async_remote_copy(
        src_ref=encoded.at[theirs, :],
        dst_ref=swap_in,
        send_sem=swap_sems.at[0],
        recv_sem=swap_sems.at[1],
        device_id={"dp": partner, "mp": me_mp},
        device_id_type=MESH,
    )
    swap.start()
    swap.wait()
    parts[me_z] = encoded[mine, :] + swap_in[...]

    z_copies = []
    for offset in range(1, pairs):
        copy = pltpu.make_async_remote_copy(
            src_ref=parts.at[me_z],
            dst_ref=parts.at[me_z],
            send_sem=z_send.at[offset],
            recv_sem=z_recv.at[offset],
            device_id={"dp": 2 * z_peer(offset) + core, "mp": me_mp},
            device_id_type=MESH,
        )
        copy.start()
        z_copies.append(copy)
    for copy in z_copies:
        copy.wait()
    total = parts[0]
    for index in range(1, pairs):
        total = total + parts[index]
    full[me_mp, core] = total * (1.0 / replicas)

    def forward(index):
        return pltpu.make_async_remote_copy(
            src_ref=full.at[index, core],
            dst_ref=full.at[index, core],
            send_sem=f_send.at[index],
            recv_sem=f_recv.at[index],
            device_id={"dp": partner, "mp": me_mp},
            device_id_type=MESH,
        )

    m_copies = []
    for offset in range(1, blocks):
        copy = pltpu.make_async_remote_copy(
            src_ref=full.at[me_mp, core],
            dst_ref=full.at[me_mp, core],
            send_sem=m_send.at[offset],
            recv_sem=m_recv.at[offset],
            device_id={"dp": me_dp, "mp": m_peer(offset)},
            device_id_type=MESH,
        )
        copy.start()
        m_copies.append(copy)
    own = forward(me_mp)
    own.start()
    own.wait()

    passed = []
    for offset in range(1, blocks):
        m_copies[offset - 1].wait()
        copy = forward(lax.rem(me_mp + blocks - offset, blocks))
        copy.start()
        passed.append(copy)
    for copy in passed:
        copy.wait()

    full_out[...] = full[...].reshape(full_out.shape)


def finish_kernel(
    replicas, blocks, full_ref, current, basis, update_ref, new_hbm, out, store_sems
):
    rows, cols = current.shape
    rank = basis.shape[1]
    chunk = cols // (2 * ITERS)
    me_dp = lax.axis_index("dp")
    me_mp = lax.axis_index("mp")

    own_rows = full_ref[pl.ds(pl.multiple_of(me_mp * rows, rows), rows), :]
    coded = own_rows.astype(jnp.bfloat16)

    def store(step):
        span = pl.ds(step * chunk, chunk)
        return pltpu.make_async_copy(
            out.at[:, span], new_hbm.at[0, :, span], store_sems.at[step]
        )

    def refresh(step):
        span = pl.ds(step * chunk, chunk)
        out[:, span] = current[:, span] - dot(coded, basis[span, :], ((1,), (1,)))

    averaged = full_ref[...]
    pair = split(averaged)
    gram = dot3(pair, pair, ((0,), (0,)))
    inverse = lax.rsqrt(jnp.full((1, 1), 1e-06, jnp.float32) + jnp.sum(averaged * averaged))
    g = gram * (inverse * inverse)
    x = own_rows * inverse
    row = lax.broadcasted_iota(jnp.int32, (rank, rank), 0)
    col = lax.broadcasted_iota(jnp.int32, (rank, rank), 1)
    diagonal = jnp.where(row == col, linear_term, 0.0)
    for index in range(ITERS):
        g_pair = split(g)
        p = diagonal + cubic_term * g + quintic_term * dot3(g_pair, g_pair)
        p_pair = split(p)
        x = dot3(split(x), p_pair)
        if index < ITERS - 1:
            g = dot3(p_pair, split(dot3(p_pair, g_pair)))
        refresh(2 * index)
        refresh(2 * index + 1)
        store(2 * index).start()
        store(2 * index + 1).start()

    band = cols // replicas
    band_basis = basis[pl.ds(pl.multiple_of(me_dp * band, 16), band), :]
    direction = dot(x.astype(jnp.bfloat16), band_basis, ((1,), (1,)))
    update_scale = math.sqrt(rows * blocks * cols / rank)
    update_ref[...] = (direction * update_scale).astype(jnp.bfloat16)
    for step in range(2 * ITERS):
        store(step).wait()


def solution(mesh):
    replicas, blocks = mesh.shape["dp"], mesh.shape["mp"]

    def body(momentum, gradient, columns):
        _, rows, cols = momentum.shape
        rank = columns.shape[0]
        chunks = cols // (BLOCK * CHUNK_BLOCKS)
        pairs = replicas // 2
        dma = pltpu.SemaphoreType.DMA
        hbm_space = pl.BlockSpec(memory_space=pltpu.HBM)
        vmem_space = pl.BlockSpec(memory_space=pltpu.VMEM)
        full, current, basis = pl.pallas_call(
            functools.partial(kernel, replicas, blocks),
            out_shape=(
                jax.ShapeDtypeStruct((blocks * rows, rank), jnp.float32),
                jax.ShapeDtypeStruct((rows, cols), jnp.float32),
                jax.ShapeDtypeStruct((cols, rank), jnp.bfloat16),
            ),
            in_specs=[hbm_space, hbm_space, vmem_space],
            out_specs=(vmem_space, vmem_space, vmem_space),
            scratch_shapes=[
                pltpu.VMEM((rows, cols), jnp.bfloat16),
                pltpu.VMEM((cols // BLOCK, rank), jnp.float32),
                pltpu.VMEM((cols // BLOCK, rank), jnp.float32),
                pltpu.VMEM((rows, rank), jnp.float32),
                pltpu.VMEM((rows // 2, rank), jnp.float32),
                pltpu.VMEM((pairs, rows // 2, rank), jnp.float32),
                pltpu.VMEM((blocks, 2, rows // 2, rank), jnp.float32),
                dma((2, chunks)),
                dma((2,)),
                dma((pairs,)),
                dma((pairs,)),
                dma((blocks,)),
                dma((blocks,)),
                dma((blocks,)),
                dma((blocks,)),
            ],
            compiler_params=pltpu.CompilerParams(
                collective_id=0, has_side_effects=True, vmem_limit_bytes=VMEM_BYTES
            ),
        )(momentum, gradient, columns.reshape(1, rank))
        return pl.pallas_call(
            functools.partial(finish_kernel, replicas, blocks),
            out_shape=(
                jax.ShapeDtypeStruct((rows, cols // replicas), jnp.bfloat16),
                jax.ShapeDtypeStruct((1, rows, cols), jnp.float32),
            ),
            in_specs=[vmem_space, vmem_space, vmem_space],
            out_specs=(vmem_space, hbm_space),
            scratch_shapes=[pltpu.VMEM((rows, cols), jnp.float32), dma((2 * ITERS,))],
            compiler_params=pltpu.CompilerParams(vmem_limit_bytes=VMEM_BYTES),
        )(full, current, basis)

    return jax.shard_map(
        body,
        mesh=mesh,
        in_specs=(P("dp", "mp", None), P("dp", "mp", None), P()),
        out_specs=(P("mp", "dp"), P("dp", "mp", None)),
        check_vma=False,
    )
```

```python
import functools
import math

import jax
import jax.numpy as jnp
from jax import lax
from jax.experimental import pallas as pl
from jax.experimental.pallas import tpu as pltpu
from jax.sharding import PartitionSpec as P

ITERS = 5
BLOCK = 64
CHUNK_BLOCKS = 8

inertia = 0.9
linear_term = 3.4445
cubic_term = -4.775
quintic_term = 2.0315
VMEM_BYTES = 24 * 2**20
MESH = pl.DeviceIdType.MESH


def cos_sin(index, period):
    quarter = period // 4
    turns = jnp.floor(index * (1.0 / quarter) + 0.5)
    angle = (index - turns * quarter) * (2.0 * math.pi / period)
    quadrant = turns - 4.0 * jnp.floor(turns * 0.25)
    x2 = angle * angle
    sine = angle * (
        1.0 + x2 * (-1.0 / 6 + x2 * (1.0 / 120 + x2 * (-1.0 / 5040 + x2 * (1.0 / 362880))))
    )
    cosine = 1.0 + x2 * (
        -0.5 + x2 * (1.0 / 24 + x2 * (-1.0 / 720 + x2 * (1.0 / 40320 - x2 * (1.0 / 3628800))))
    )
    odd = (quadrant == 1.0) | (quadrant == 3.0)
    cos_part = jnp.where(odd, sine, cosine)
    sin_part = jnp.where(odd, cosine, sine)
    cos_out = jnp.where((quadrant == 1.0) | (quadrant == 2.0), -cos_part, cos_part)
    sin_out = jnp.where(quadrant >= 2.0, -sin_part, sin_part)
    return cos_out, sin_out


def split(x):
    high = x.astype(jnp.bfloat16)
    return high, (x - high.astype(jnp.float32)).astype(jnp.bfloat16)


def dot(a, b, dims=((1,), (0,))):
    return lax.dot_general(a, b, (dims, ((), ())), preferred_element_type=jnp.float32)


def dot3(a, b, dims=((1,), (0,))):
    return dot(a[0], b[0], dims) + dot(a[0], b[1], dims) + dot(a[1], b[0], dims)


def kernel(
    replicas,
    blocks,
    momentum_hbm,
    gradient_hbm,
    columns_hbm,
    full_out,
    current,
    basis,
    columns_ref,
    grad,
    cos_high,
    sin_high,
    encoded,
    swap_in,
    parts,
    full,
    columns_sem,
    load_sems,
    swap_sems,
    z_send,
    z_recv,
    m_send,
    m_recv,
    f_send,
    f_recv,
):
    rows, cols = current.shape
    rank = basis.shape[1]
    half = rows // 2
    pairs = replicas // 2
    chunk = BLOCK * CHUNK_BLOCKS
    chunks = cols // chunk
    me_dp = lax.axis_index("dp")
    me_mp = lax.axis_index("mp")
    core = lax.rem(me_dp, 2)
    me_z = lax.div(me_dp, 2)
    partner = me_dp + 1 - 2 * core

    def load(step):
        span = pl.ds(pl.multiple_of(step * chunk, chunk), chunk)
        return (
            pltpu.make_async_copy(
                momentum_hbm.at[0, :, span], current.at[:, span], load_sems.at[0, step]
            ),
            pltpu.make_async_copy(
                gradient_hbm.at[0, :, span], grad.at[:, span], load_sems.at[1, step]
            ),
        )

    columns_copy = pltpu.make_async_copy(columns_hbm, columns_ref, columns_sem)
    columns_copy.start()
    for step in range(chunks):
        for copy in load(step):
            copy.start()

    def z_peer(offset):
        return lax.rem(me_z + offset, pairs)

    def m_peer(offset):
        return lax.rem(me_mp + offset, blocks)

    barrier = pltpu.get_barrier_semaphore()
    pl.semaphore_signal(
        barrier, inc=1, device_id={"dp": partner, "mp": me_mp}, device_id_type=MESH
    )
    for offset in range(1, pairs):
        pl.semaphore_signal(
            barrier,
            inc=1,
            device_id={"dp": 2 * z_peer(offset) + core, "mp": me_mp},
            device_id_type=MESH,
        )
    for offset in range(1, blocks):
        pl.semaphore_signal(
            barrier,
            inc=1,
            device_id={"dp": me_dp, "mp": m_peer(offset)},
            device_id_type=MESH,
        )

    columns_copy.wait()
    frequency = columns_ref[...].astype(jnp.float32)
    scale = jnp.where(columns_ref[...] == 0, math.sqrt(1.0 / cols), math.sqrt(2.0 / cols))
    high_count = cos_high.shape[0]
    high_index = lax.broadcasted_iota(jnp.int32, (high_count, rank), 0).astype(jnp.float32)
    ch, sh = cos_sin(high_index * frequency, 2 * cols // BLOCK)
    cos_high[...] = ch
    sin_high[...] = sh
    low_index = lax.broadcasted_iota(jnp.int32, (BLOCK, rank), 0).astype(jnp.float32)
    cl, sl = cos_sin((2.0 * low_index + 1.0) * frequency, 4 * cols)
    cl = cl * scale
    sl = sl * scale

    encoded[...] = jnp.zeros_like(encoded)

    def encode(step, carry):
        for block in range(CHUNK_BLOCKS):
            index = step * CHUNK_BLOCKS + block
            table = cos_high[pl.ds(index, 1), :] * cl - sin_high[pl.ds(index, 1), :] * sl
            start = pl.multiple_of(index * BLOCK, BLOCK)
            basis[pl.ds(start, BLOCK), :] = table.astype(jnp.bfloat16)
        for copy in load(step):
            copy.wait()
        span = pl.ds(pl.multiple_of(step * chunk, chunk), chunk)
        now = inertia * current[:, span] + grad[:, span].astype(jnp.float32)
        current[:, span] = now
        encoded[...] += dot(now.astype(jnp.bfloat16), basis[span, :])
        return carry

    lax.fori_loop(0, chunks, encode, 0)

    pl.semaphore_wait(barrier, 1 + (pairs - 1) + (blocks - 1))

    mine = pl.ds(pl.multiple_of(core * half, half), half)
    theirs = pl.ds(pl.multiple_of((1 - core) * half, half), half)
    swap = pltpu.make_async_remote_copy(
        src_ref=encoded.at[theirs, :],
        dst_ref=swap_in,
        send_sem=swap_sems.at[0],
        recv_sem=swap_sems.at[1],
        device_id={"dp": partner, "mp": me_mp},
        device_id_type=MESH,
    )
    swap.start()
    swap.wait()
    parts[me_z] = encoded[mine, :] + swap_in[...]

    z_copies = []
    for offset in range(1, pairs):
        copy = pltpu.make_async_remote_copy(
            src_ref=parts.at[me_z],
            dst_ref=parts.at[me_z],
            send_sem=z_send.at[offset],
            recv_sem=z_recv.at[offset],
            device_id={"dp": 2 * z_peer(offset) + core, "mp": me_mp},
            device_id_type=MESH,
        )
        copy.start()
        z_copies.append(copy)
    for copy in z_copies:
        copy.wait()
    total = parts[0]
    for index in range(1, pairs):
        total = total + parts[index]
    full[me_mp, core] = total * (1.0 / replicas)

    def forward(index):
        return pltpu.make_async_remote_copy(
            src_ref=full.at[index, core],
            dst_ref=full.at[index, core],
            send_sem=f_send.at[index],
            recv_sem=f_recv.at[index],
            device_id={"dp": partner, "mp": me_mp},
            device_id_type=MESH,
        )

    m_copies = []
    for offset in range(1, blocks):
        copy = pltpu.make_async_remote_copy(
            src_ref=full.at[me_mp, core],
            dst_ref=full.at[me_mp, core],
            send_sem=m_send.at[offset],
            recv_sem=m_recv.at[offset],
            device_id={"dp": me_dp, "mp": m_peer(offset)},
            device_id_type=MESH,
        )
        copy.start()
        m_copies.append(copy)
    own = forward(me_mp)
    own.start()
    own.wait()

    passed = []
    for offset in range(1, blocks):
        m_copies[offset - 1].wait()
        copy = forward(lax.rem(me_mp + blocks - offset, blocks))
        copy.start()
        passed.append(copy)
    for copy in passed:
        copy.wait()

    full_out[...] = full[...].reshape(full_out.shape)


def finish_kernel(
    replicas, blocks, full_ref, current, basis, update_ref, new_hbm, out, store_sems
):
    rows, cols = current.shape
    rank = basis.shape[1]
    chunk = cols // (2 * ITERS)
    me_dp = lax.axis_index("dp")
    me_mp = lax.axis_index("mp")

    own_rows = full_ref[pl.ds(pl.multiple_of(me_mp * rows, rows), rows), :]
    coded = own_rows.astype(jnp.bfloat16)

    def store(step):
        span = pl.ds(step * chunk, chunk)
        return pltpu.make_async_copy(
            out.at[:, span], new_hbm.at[0, :, span], store_sems.at[step]
        )

    def refresh(step):
        span = pl.ds(step * chunk, chunk)
        out[:, span] = current[:, span] - dot(coded, basis[span, :], ((1,), (1,)))

    averaged = full_ref[...]
    pair = split(averaged)
    gram = dot3(pair, pair, ((0,), (0,)))
    inverse = lax.rsqrt(jnp.full((1, 1), 1e-06, jnp.float32) + jnp.sum(averaged * averaged))
    g = gram * (inverse * inverse)
    x = own_rows * inverse
    row = lax.broadcasted_iota(jnp.int32, (rank, rank), 0)
    col = lax.broadcasted_iota(jnp.int32, (rank, rank), 1)
    diagonal = jnp.where(row == col, linear_term, 0.0)
    for index in range(ITERS):
        g_pair = split(g)
        p = diagonal + cubic_term * g + quintic_term * dot3(g_pair, g_pair)
        p_pair = split(p)
        x = dot3(split(x), p_pair)
        if index < ITERS - 1:
            g = dot3(p_pair, split(dot3(p_pair, g_pair)))
        refresh(2 * index)
        refresh(2 * index + 1)
        store(2 * index).start()
        store(2 * index + 1).start()

    band = cols // replicas
    band_basis = basis[pl.ds(pl.multiple_of(me_dp * band, 16), band), :]
    direction = dot(x.astype(jnp.bfloat16), band_basis, ((1,), (1,)))
    update_scale = math.sqrt(rows * blocks * cols / rank)
    update_ref[...] = (direction * update_scale).astype(jnp.bfloat16)
    for step in range(2 * ITERS):
        store(step).wait()


def solution(mesh):
    replicas, blocks = mesh.shape["dp"], mesh.shape["mp"]

    def body(momentum, gradient, columns):
        _, rows, cols = momentum.shape
        rank = columns.shape[0]
        chunks = cols // (BLOCK * CHUNK_BLOCKS)
        pairs = replicas // 2
        dma = pltpu.SemaphoreType.DMA
        hbm_space = pl.BlockSpec(memory_space=pltpu.HBM)
        vmem_space = pl.BlockSpec(memory_space=pltpu.VMEM)
        full, current, basis = pl.pallas_call(
            functools.partial(kernel, replicas, blocks),
            out_shape=(
                jax.ShapeDtypeStruct((blocks * rows, rank), jnp.float32),
                jax.ShapeDtypeStruct((rows, cols), jnp.float32),
                jax.ShapeDtypeStruct((cols, rank), jnp.bfloat16),
            ),
            in_specs=[hbm_space, hbm_space, hbm_space],
            out_specs=(vmem_space, vmem_space, vmem_space),
            scratch_shapes=[
                pltpu.VMEM((1, rank), jnp.int32),
                pltpu.VMEM((rows, cols), jnp.bfloat16),
                pltpu.VMEM((cols // BLOCK, rank), jnp.float32),
                pltpu.VMEM((cols // BLOCK, rank), jnp.float32),
                pltpu.VMEM((rows, rank), jnp.float32),
                pltpu.VMEM((rows // 2, rank), jnp.float32),
                pltpu.VMEM((pairs, rows // 2, rank), jnp.float32),
                pltpu.VMEM((blocks, 2, rows // 2, rank), jnp.float32),
                dma,
                dma((2, chunks)),
                dma((2,)),
                dma((pairs,)),
                dma((pairs,)),
                dma((blocks,)),
                dma((blocks,)),
                dma((blocks,)),
                dma((blocks,)),
            ],
            compiler_params=pltpu.CompilerParams(
                collective_id=0, has_side_effects=True, vmem_limit_bytes=VMEM_BYTES
            ),
        )(
            pltpu.with_memory_space_constraint(momentum, pltpu.HBM),
            pltpu.with_memory_space_constraint(gradient, pltpu.HBM),
            pltpu.with_memory_space_constraint(columns.reshape(1, rank), pltpu.HBM),
        )
        return pl.pallas_call(
            functools.partial(finish_kernel, replicas, blocks),
            out_shape=(
                jax.ShapeDtypeStruct((rows, cols // replicas), jnp.bfloat16),
                jax.ShapeDtypeStruct((1, rows, cols), jnp.float32),
            ),
            in_specs=[vmem_space, vmem_space, vmem_space],
            out_specs=(vmem_space, hbm_space),
            scratch_shapes=[pltpu.VMEM((rows, cols), jnp.float32), dma((2 * ITERS,))],
            compiler_params=pltpu.CompilerParams(vmem_limit_bytes=VMEM_BYTES),
        )(full, current, basis)

    return jax.shard_map(
        body,
        mesh=mesh,
        in_specs=(P("dp", "mp", None), P("dp", "mp", None), P()),
        out_specs=(P("mp", "dp"), P("dp", "mp", None)),
        check_vma=False,
    )
```

```python
import functools
import math

import jax
import jax.numpy as jnp
from jax import lax
from jax.experimental import pallas as pl
from jax.experimental.pallas import tpu as pltpu
from jax.sharding import PartitionSpec as P

ITERS = 5
BLOCK = 64
CHUNK_BLOCKS = 8

inertia = 0.9
linear_term = 3.4445
cubic_term = -4.775
quintic_term = 2.0315
SPLIT = 2
VMEM_BYTES = 24 * 2**20
MESH = pl.DeviceIdType.MESH


def cos_sin(index, period):
    quarter = period // 4
    turns = jnp.floor(index * (1.0 / quarter) + 0.5)
    angle = (index - turns * quarter) * (2.0 * math.pi / period)
    quadrant = turns - 4.0 * jnp.floor(turns * 0.25)
    x2 = angle * angle
    sine = angle * (
        1.0 + x2 * (-1.0 / 6 + x2 * (1.0 / 120 + x2 * (-1.0 / 5040 + x2 * (1.0 / 362880))))
    )
    cosine = 1.0 + x2 * (
        -0.5 + x2 * (1.0 / 24 + x2 * (-1.0 / 720 + x2 * (1.0 / 40320 - x2 * (1.0 / 3628800))))
    )
    odd = (quadrant == 1.0) | (quadrant == 3.0)
    cos_part = jnp.where(odd, sine, cosine)
    sin_part = jnp.where(odd, cosine, sine)
    cos_out = jnp.where((quadrant == 1.0) | (quadrant == 2.0), -cos_part, cos_part)
    sin_out = jnp.where(quadrant >= 2.0, -sin_part, sin_part)
    return cos_out, sin_out


def peer(me, step, count, back=False):
    if count & (count - 1):
        return lax.rem(me + (count - step if back else step), count)
    there, bit = me, 1
    while bit < count:
        if step & bit:
            there = there + bit - 2 * bit * lax.rem(lax.div(me, bit), 2)
        bit *= 2
    return there


def split(x):
    high = x.astype(jnp.bfloat16)
    return high, (x - high.astype(jnp.float32)).astype(jnp.bfloat16)


def dot(a, b, dims=((1,), (0,))):
    return lax.dot_general(a, b, (dims, ((), ())), preferred_element_type=jnp.float32)


def dot3(a, b, dims=((1,), (0,))):
    return dot(a[0], b[0], dims) + dot(a[0], b[1], dims) + dot(a[1], b[0], dims)


def kernel(
    replicas,
    blocks,
    momentum_hbm,
    gradient_hbm,
    columns_hbm,
    full_out,
    current,
    basis,
    columns_ref,
    grad,
    cos_high,
    sin_high,
    encoded,
    swap_in,
    parts,
    full,
    columns_sem,
    load_sems,
    swap_sems,
    z_send,
    z_recv,
    m_send,
    m_recv,
    f_send,
    f_recv,
):
    rows, cols = current.shape
    rank = basis.shape[1]
    half = rows // 2
    pairs = replicas // 2
    chunk = BLOCK * CHUNK_BLOCKS
    chunks = cols // chunk
    me_dp = lax.axis_index("dp")
    me_mp = lax.axis_index("mp")
    core = lax.rem(me_dp, 2)
    me_z = lax.div(me_dp, 2)
    partner = me_dp + 1 - 2 * core

    def load(step):
        span = pl.ds(pl.multiple_of(step * chunk, chunk), chunk)
        return (
            pltpu.make_async_copy(
                momentum_hbm.at[0, :, span], current.at[:, span], load_sems.at[0, step]
            ),
            pltpu.make_async_copy(
                gradient_hbm.at[0, :, span], grad.at[:, span], load_sems.at[1, step]
            ),
        )

    columns_copy = pltpu.make_async_copy(columns_hbm, columns_ref, columns_sem)
    columns_copy.start()
    for step in range(chunks):
        for copy in load(step):
            copy.start()

    def z_peer(step):
        return peer(me_z, step, pairs)

    def m_peer(step):
        return peer(me_mp, step, blocks)

    def m_source(step):
        return peer(me_mp, step, blocks, back=True)

    barrier = pltpu.get_barrier_semaphore()
    pl.semaphore_signal(
        barrier, inc=1, device_id={"dp": partner, "mp": me_mp}, device_id_type=MESH
    )
    for offset in range(1, pairs):
        pl.semaphore_signal(
            barrier,
            inc=1,
            device_id={"dp": 2 * z_peer(offset) + core, "mp": me_mp},
            device_id_type=MESH,
        )
    for offset in range(1, blocks):
        pl.semaphore_signal(
            barrier,
            inc=1,
            device_id={"dp": me_dp, "mp": m_peer(offset)},
            device_id_type=MESH,
        )

    columns_copy.wait()
    frequency = columns_ref[...].astype(jnp.float32)
    scale = jnp.where(columns_ref[...] == 0, math.sqrt(1.0 / cols), math.sqrt(2.0 / cols))
    high_count = cos_high.shape[0]
    high_index = lax.broadcasted_iota(jnp.int32, (high_count, rank), 0).astype(jnp.float32)
    ch, sh = cos_sin(high_index * frequency, 2 * cols // BLOCK)
    cos_high[...] = ch
    sin_high[...] = sh
    low_index = lax.broadcasted_iota(jnp.int32, (BLOCK, rank), 0).astype(jnp.float32)
    cl, sl = cos_sin((2.0 * low_index + 1.0) * frequency, 4 * cols)
    cl = cl * scale
    sl = sl * scale

    encoded[...] = jnp.zeros_like(encoded)

    def encode(step, carry):
        for block in range(CHUNK_BLOCKS):
            index = step * CHUNK_BLOCKS + block
            table = cos_high[pl.ds(index, 1), :] * cl - sin_high[pl.ds(index, 1), :] * sl
            start = pl.multiple_of(index * BLOCK, BLOCK)
            basis[pl.ds(start, BLOCK), :] = table.astype(jnp.bfloat16)
        for copy in load(step):
            copy.wait()
        span = pl.ds(pl.multiple_of(step * chunk, chunk), chunk)
        now = inertia * current[:, span] + grad[:, span].astype(jnp.float32)
        current[:, span] = now
        encoded[...] += dot(now.astype(jnp.bfloat16), basis[span, :])
        return carry

    lax.fori_loop(0, chunks, encode, 0)

    pl.semaphore_wait(barrier, 1 + (pairs - 1) + (blocks - 1))

    piece = half // SPLIT
    sends = []

    def send(src, dst, send_sem, recv_sem, dp, mp):
        copy = pltpu.make_async_remote_copy(
            src_ref=src,
            dst_ref=dst,
            send_sem=send_sem,
            recv_sem=recv_sem,
            device_id={"dp": dp, "mp": mp},
            device_id_type=MESH,
        )
        copy.start()
        sends.append(copy)
        return copy

    def rows_of(owner, part):
        return pl.ds(pl.multiple_of(owner * half + part * piece, piece), piece)

    swaps = [
        send(
            encoded.at[rows_of(1 - core, part), :],
            swap_in.at[part],
            swap_sems.at[0, part],
            swap_sems.at[1, part],
            partner,
            me_mp,
        )
        for part in range(SPLIT)
    ]

    z_copies = []
    for part in range(SPLIT):
        swaps[part].wait_recv()
        parts[part, me_z] = encoded[rows_of(core, part), :] + swap_in[part]
        z_copies.append(
            [
                send(
                    parts.at[part, me_z],
                    parts.at[part, me_z],
                    z_send.at[part, step],
                    z_recv.at[part, step],
                    2 * z_peer(step) + core,
                    me_mp,
                )
                for step in range(pairs - 1, 0, -1)
            ]
        )

    passed = []

    def forward(index, part):
        place = full.at[index, core, part]
        passed.append(
            send(place, place, f_send.at[part, index], f_recv.at[part, index], partner, me_mp)
        )

    m_copies = []
    for part in range(SPLIT):
        for copy in z_copies[part]:
            copy.wait_recv()
        total = parts[part, 0]
        for index in range(1, pairs):
            total = total + parts[part, index]
        full[me_mp, core, part] = total * (1.0 / replicas)
        place = full.at[me_mp, core, part]
        m_copies.append(
            [
                send(
                    place,
                    place,
                    m_send.at[part, step],
                    m_recv.at[part, step],
                    me_dp,
                    m_peer(step),
                )
                for step in range(blocks - 1, 0, -1)
            ]
        )
        forward(me_mp, part)
    for part in range(SPLIT):
        for step in range(1, blocks):
            m_copies[part][blocks - 1 - step].wait_recv()
            forward(m_source(step), part)
    for copy in passed:
        copy.wait_recv()
    for copy in sends:
        copy.wait_send()
    full_out[...] = full[...].reshape(full_out.shape)


def finish_kernel(
    replicas, blocks, full_ref, current, basis, update_ref, new_hbm, out, store_sems
):
    rows, cols = current.shape
    rank = basis.shape[1]
    chunk = cols // (2 * ITERS)
    me_dp = lax.axis_index("dp")
    me_mp = lax.axis_index("mp")

    own_rows = full_ref[pl.ds(pl.multiple_of(me_mp * rows, rows), rows), :]
    coded = own_rows.astype(jnp.bfloat16)

    def store(step):
        span = pl.ds(step * chunk, chunk)
        return pltpu.make_async_copy(
            out.at[:, span], new_hbm.at[0, :, span], store_sems.at[step]
        )

    def refresh(step):
        span = pl.ds(step * chunk, chunk)
        out[:, span] = current[:, span] - dot(coded, basis[span, :], ((1,), (1,)))

    averaged = full_ref[...]
    pair = split(averaged)
    gram = dot3(pair, pair, ((0,), (0,)))
    inverse = lax.rsqrt(jnp.full((1, 1), 1e-06, jnp.float32) + jnp.sum(averaged * averaged))
    g = gram * (inverse * inverse)
    x = own_rows * inverse
    row = lax.broadcasted_iota(jnp.int32, (rank, rank), 0)
    col = lax.broadcasted_iota(jnp.int32, (rank, rank), 1)
    diagonal = jnp.where(row == col, linear_term, 0.0)
    for index in range(ITERS):
        g_pair = split(g)
        p = diagonal + cubic_term * g + quintic_term * dot3(g_pair, g_pair)
        p_pair = split(p)
        x = dot3(split(x), p_pair)
        if index < ITERS - 1:
            g = dot3(p_pair, split(dot3(p_pair, g_pair)))
        refresh(2 * index)
        refresh(2 * index + 1)
        store(2 * index).start()
        store(2 * index + 1).start()

    band = cols // replicas
    band_basis = basis[pl.ds(pl.multiple_of(me_dp * band, 16), band), :]
    direction = dot(x.astype(jnp.bfloat16), band_basis, ((1,), (1,)))
    update_scale = math.sqrt(rows * blocks * cols / rank)
    update_ref[...] = (direction * update_scale).astype(jnp.bfloat16)
    for step in range(2 * ITERS):
        store(step).wait()


def solution(mesh):
    replicas, blocks = mesh.shape["dp"], mesh.shape["mp"]

    def body(momentum, gradient, columns):
        _, rows, cols = momentum.shape
        rank = columns.shape[0]
        chunks = cols // (BLOCK * CHUNK_BLOCKS)
        pairs = replicas // 2
        piece = rows // 2 // SPLIT
        dma = pltpu.SemaphoreType.DMA
        hbm_space = pl.BlockSpec(memory_space=pltpu.HBM)
        vmem_space = pl.BlockSpec(memory_space=pltpu.VMEM)
        full, current, basis = pl.pallas_call(
            functools.partial(kernel, replicas, blocks),
            out_shape=(
                jax.ShapeDtypeStruct((blocks * rows, rank), jnp.float32),
                jax.ShapeDtypeStruct((rows, cols), jnp.float32),
                jax.ShapeDtypeStruct((cols, rank), jnp.bfloat16),
            ),
            in_specs=[hbm_space, hbm_space, hbm_space],
            out_specs=(vmem_space, vmem_space, vmem_space),
            scratch_shapes=[
                pltpu.VMEM((1, rank), jnp.int32),
                pltpu.VMEM((rows, cols), jnp.bfloat16),
                pltpu.VMEM((cols // BLOCK, rank), jnp.float32),
                pltpu.VMEM((cols // BLOCK, rank), jnp.float32),
                pltpu.VMEM((rows, rank), jnp.float32),
                pltpu.VMEM((SPLIT, piece, rank), jnp.float32),
                pltpu.VMEM((SPLIT, pairs, piece, rank), jnp.float32),
                pltpu.VMEM((blocks, 2, SPLIT, piece, rank), jnp.float32),
                dma,
                dma((2, chunks)),
                dma((2, SPLIT)),
                dma((SPLIT, pairs)),
                dma((SPLIT, pairs)),
                dma((SPLIT, blocks)),
                dma((SPLIT, blocks)),
                dma((SPLIT, blocks)),
                dma((SPLIT, blocks)),
            ],
            compiler_params=pltpu.CompilerParams(
                collective_id=0, has_side_effects=True, vmem_limit_bytes=VMEM_BYTES
            ),
        )(
            pltpu.with_memory_space_constraint(momentum, pltpu.HBM),
            pltpu.with_memory_space_constraint(gradient, pltpu.HBM),
            pltpu.with_memory_space_constraint(columns.reshape(1, rank), pltpu.HBM),
        )
        return pl.pallas_call(
            functools.partial(finish_kernel, replicas, blocks),
            out_shape=(
                jax.ShapeDtypeStruct((rows, cols // replicas), jnp.bfloat16),
                jax.ShapeDtypeStruct((1, rows, cols), jnp.float32),
            ),
            in_specs=[vmem_space, vmem_space, vmem_space],
            out_specs=(vmem_space, hbm_space),
            scratch_shapes=[pltpu.VMEM((rows, cols), jnp.float32), dma((2 * ITERS,))],
            compiler_params=pltpu.CompilerParams(vmem_limit_bytes=VMEM_BYTES),
        )(full, current, basis)

    return jax.shard_map(
        body,
        mesh=mesh,
        in_specs=(P("dp", "mp", None), P("dp", "mp", None), P()),
        out_specs=(P("mp", "dp"), P("dp", "mp", None)),
        check_vma=False,
    )
```

```python
import functools
import math

import jax
import jax.numpy as jnp
from jax import lax
from jax.experimental import pallas as pl
from jax.experimental.pallas import tpu as pltpu
from jax.sharding import PartitionSpec as P

ITERS = 5
BLOCK = 64
CHUNK_BLOCKS = 40

inertia = 0.9
linear_term = 3.4445
cubic_term = -4.775
quintic_term = 2.0315
VMEM_BYTES = 24 * 2**20
MESH = pl.DeviceIdType.MESH


def cos_sin(index, period):
    quarter = period // 4
    turns = jnp.floor(index * (1.0 / quarter) + 0.5)
    angle = (index - turns * quarter) * (2.0 * math.pi / period)
    quadrant = turns - 4.0 * jnp.floor(turns * 0.25)
    x2 = angle * angle
    sine = angle * (
        1.0 + x2 * (-1.0 / 6 + x2 * (1.0 / 120 + x2 * (-1.0 / 5040 + x2 * (1.0 / 362880))))
    )
    cosine = 1.0 + x2 * (
        -0.5 + x2 * (1.0 / 24 + x2 * (-1.0 / 720 + x2 * (1.0 / 40320 - x2 * (1.0 / 3628800))))
    )
    odd = (quadrant == 1.0) | (quadrant == 3.0)
    cos_part = jnp.where(odd, sine, cosine)
    sin_part = jnp.where(odd, cosine, sine)
    cos_out = jnp.where((quadrant == 1.0) | (quadrant == 2.0), -cos_part, cos_part)
    sin_out = jnp.where(quadrant >= 2.0, -sin_part, sin_part)
    return cos_out, sin_out


def split(x):
    high = x.astype(jnp.bfloat16)
    return high, (x - high.astype(jnp.float32)).astype(jnp.bfloat16)


def dot(a, b, dims=((1,), (0,))):
    return lax.dot_general(a, b, (dims, ((), ())), preferred_element_type=jnp.float32)


def dot3(a, b, dims=((1,), (0,))):
    (i,), (j,) = dims
    return dot(
        jnp.concatenate([a[0], a[0], a[1]], axis=i), jnp.concatenate([b[0], b[1], b[0]], axis=j), dims
    )


def kernel(
    replicas,
    blocks,
    momentum_hbm,
    gradient_hbm,
    columns_hbm,
    full_out,
    current,
    basis,
    columns_ref,
    grad,
    cos_high,
    sin_high,
    encoded,
    swap_in,
    parts,
    full,
    columns_sem,
    load_sems,
    swap_sems,
    z_send,
    z_recv,
    m_send,
    m_recv,
    f_send,
    f_recv,
):
    rows, cols = current.shape
    rank = basis.shape[1]
    half = rows // 2
    pairs = replicas // 2
    chunk = BLOCK * CHUNK_BLOCKS
    chunks = cols // chunk
    me_dp = lax.axis_index("dp")
    me_mp = lax.axis_index("mp")
    core = lax.rem(me_dp, 2)
    me_z = lax.div(me_dp, 2)
    partner = me_dp + 1 - 2 * core

    def load(step):
        span = pl.ds(pl.multiple_of(step * chunk, chunk), chunk)
        return (
            pltpu.make_async_copy(
                momentum_hbm.at[0, :, span], current.at[:, span], load_sems.at[0, step]
            ),
            pltpu.make_async_copy(
                gradient_hbm.at[0, :, span], grad.at[:, span], load_sems.at[1, step]
            ),
        )

    columns_copy = pltpu.make_async_copy(columns_hbm, columns_ref, columns_sem)
    columns_copy.start()
    for step in range(chunks):
        for copy in load(step):
            copy.start()

    def z_peer(offset):
        return lax.rem(me_z + offset, pairs)

    def m_peer(offset):
        return lax.rem(me_mp + offset, blocks)

    barrier = pltpu.get_barrier_semaphore()
    pl.semaphore_signal(
        barrier, inc=1, device_id={"dp": partner, "mp": me_mp}, device_id_type=MESH
    )
    for offset in range(1, pairs):
        pl.semaphore_signal(
            barrier,
            inc=1,
            device_id={"dp": 2 * z_peer(offset) + core, "mp": me_mp},
            device_id_type=MESH,
        )
    for offset in range(1, blocks):
        pl.semaphore_signal(
            barrier,
            inc=1,
            device_id={"dp": me_dp, "mp": m_peer(offset)},
            device_id_type=MESH,
        )

    columns_copy.wait()
    frequency = columns_ref[...].astype(jnp.float32)
    scale = jnp.where(columns_ref[...] == 0, math.sqrt(1.0 / cols), math.sqrt(2.0 / cols))
    high_count = cos_high.shape[0]
    high_index = lax.broadcasted_iota(jnp.int32, (high_count, rank), 0).astype(jnp.float32)
    ch, sh = cos_sin(high_index * frequency, 2 * cols // BLOCK)
    cos_high[...] = ch
    sin_high[...] = sh
    low_index = lax.broadcasted_iota(jnp.int32, (BLOCK, rank), 0).astype(jnp.float32)
    cl, sl = cos_sin((2.0 * low_index + 1.0) * frequency, 4 * cols)
    cl = cl * scale
    sl = sl * scale

    encoded[...] = jnp.zeros_like(encoded)

    def encode(step, carry):
        for block in range(CHUNK_BLOCKS):
            index = step * CHUNK_BLOCKS + block
            table = cos_high[pl.ds(index, 1), :] * cl - sin_high[pl.ds(index, 1), :] * sl
            start = pl.multiple_of(index * BLOCK, BLOCK)
            basis[pl.ds(start, BLOCK), :] = table.astype(jnp.bfloat16)
        for copy in load(step):
            copy.wait()
        span = pl.ds(pl.multiple_of(step * chunk, chunk), chunk)
        now = inertia * current[:, span] + grad[:, span].astype(jnp.float32)
        current[:, span] = now
        encoded[...] += dot(now.astype(jnp.bfloat16), basis[span, :])
        return carry

    lax.fori_loop(0, chunks, encode, 0)

    pl.semaphore_wait(barrier, 1 + (pairs - 1) + (blocks - 1))

    mine = pl.ds(pl.multiple_of(core * half, half), half)
    theirs = pl.ds(pl.multiple_of((1 - core) * half, half), half)
    swap = pltpu.make_async_remote_copy(
        src_ref=encoded.at[theirs, :],
        dst_ref=swap_in,
        send_sem=swap_sems.at[0],
        recv_sem=swap_sems.at[1],
        device_id={"dp": partner, "mp": me_mp},
        device_id_type=MESH,
    )
    swap.start()
    swap.wait()
    parts[me_z] = encoded[mine, :] + swap_in[...]

    z_copies = []
    for offset in range(1, pairs):
        copy = pltpu.make_async_remote_copy(
            src_ref=parts.at[me_z],
            dst_ref=parts.at[me_z],
            send_sem=z_send.at[offset],
            recv_sem=z_recv.at[offset],
            device_id={"dp": 2 * z_peer(offset) + core, "mp": me_mp},
            device_id_type=MESH,
        )
        copy.start()
        z_copies.append(copy)
    for copy in z_copies:
        copy.wait()
    total = parts[0]
    for index in range(1, pairs):
        total = total + parts[index]
    full[me_mp, core] = total * (1.0 / replicas)

    def forward(index):
        return pltpu.make_async_remote_copy(
            src_ref=full.at[index, core],
            dst_ref=full.at[index, core],
            send_sem=f_send.at[index],
            recv_sem=f_recv.at[index],
            device_id={"dp": partner, "mp": me_mp},
            device_id_type=MESH,
        )

    m_copies = []
    for offset in range(1, blocks):
        copy = pltpu.make_async_remote_copy(
            src_ref=full.at[me_mp, core],
            dst_ref=full.at[me_mp, core],
            send_sem=m_send.at[offset],
            recv_sem=m_recv.at[offset],
            device_id={"dp": me_dp, "mp": m_peer(offset)},
            device_id_type=MESH,
        )
        copy.start()
        m_copies.append(copy)
    own = forward(me_mp)
    own.start()
    own.wait()

    passed = []
    for offset in range(1, blocks):
        m_copies[offset - 1].wait()
        copy = forward(lax.rem(me_mp + blocks - offset, blocks))
        copy.start()
        passed.append(copy)
    for copy in passed:
        copy.wait()

    full_out[...] = full[...].reshape(full_out.shape)


def finish_kernel(
    replicas, blocks, full_ref, current, basis, update_ref, new_hbm, out, store_sems
):
    rows, cols = current.shape
    rank = basis.shape[1]
    chunk = cols // (2 * ITERS)
    me_dp = lax.axis_index("dp")
    me_mp = lax.axis_index("mp")

    own_rows = full_ref[pl.ds(pl.multiple_of(me_mp * rows, rows), rows), :]
    coded = own_rows.astype(jnp.bfloat16)

    def store(step):
        span = pl.ds(step * chunk, chunk)
        return pltpu.make_async_copy(
            out.at[:, span], new_hbm.at[0, :, span], store_sems.at[step]
        )

    def refresh(step):
        span = pl.ds(step * chunk, chunk)
        out[:, span] = current[:, span] - dot(coded, basis[span, :], ((1,), (1,)))

    averaged = full_ref[...]
    pair = split(averaged)
    gram = dot3(pair, pair, ((0,), (0,)))
    inverse = lax.rsqrt(jnp.full((1, 1), 1e-06, jnp.float32) + jnp.sum(averaged * averaged))
    g = gram * (inverse * inverse)
    x = own_rows * inverse
    row = lax.broadcasted_iota(jnp.int32, (rank, rank), 0)
    col = lax.broadcasted_iota(jnp.int32, (rank, rank), 1)
    diagonal = jnp.where(row == col, linear_term, 0.0)
    for index in range(ITERS):
        g_pair = split(g)
        p = diagonal + cubic_term * g + quintic_term * dot3(g_pair, g_pair)
        p_pair = split(p)
        x = dot3(split(x), p_pair)
        if index < ITERS - 1:
            g = dot3(p_pair, split(dot3(p_pair, g_pair)))
        refresh(2 * index)
        refresh(2 * index + 1)
        store(2 * index).start()
        store(2 * index + 1).start()

    band = cols // replicas
    band_basis = basis[pl.ds(pl.multiple_of(me_dp * band, 16), band), :]
    direction = dot(x.astype(jnp.bfloat16), band_basis, ((1,), (1,)))
    update_scale = math.sqrt(rows * blocks * cols / rank)
    update_ref[...] = (direction * update_scale).astype(jnp.bfloat16)
    for step in range(2 * ITERS):
        store(step).wait()


def solution(mesh):
    replicas, blocks = mesh.shape["dp"], mesh.shape["mp"]

    def body(momentum, gradient, columns):
        _, rows, cols = momentum.shape
        rank = columns.shape[0]
        chunks = cols // (BLOCK * CHUNK_BLOCKS)
        pairs = replicas // 2
        dma = pltpu.SemaphoreType.DMA
        hbm_space = pl.BlockSpec(memory_space=pltpu.HBM)
        vmem_space = pl.BlockSpec(memory_space=pltpu.VMEM)
        full, current, basis = pl.pallas_call(
            functools.partial(kernel, replicas, blocks),
            out_shape=(
                jax.ShapeDtypeStruct((blocks * rows, rank), jnp.float32),
                jax.ShapeDtypeStruct((rows, cols), jnp.float32),
                jax.ShapeDtypeStruct((cols, rank), jnp.bfloat16),
            ),
            in_specs=[hbm_space, hbm_space, hbm_space],
            out_specs=(vmem_space, vmem_space, vmem_space),
            scratch_shapes=[
                pltpu.VMEM((1, rank), jnp.int32),
                pltpu.VMEM((rows, cols), jnp.bfloat16),
                pltpu.VMEM((cols // BLOCK, rank), jnp.float32),
                pltpu.VMEM((cols // BLOCK, rank), jnp.float32),
                pltpu.VMEM((rows, rank), jnp.float32),
                pltpu.VMEM((rows // 2, rank), jnp.float32),
                pltpu.VMEM((pairs, rows // 2, rank), jnp.float32),
                pltpu.VMEM((blocks, 2, rows // 2, rank), jnp.float32),
                dma,
                dma((2, chunks)),
                dma((2,)),
                dma((pairs,)),
                dma((pairs,)),
                dma((blocks,)),
                dma((blocks,)),
                dma((blocks,)),
                dma((blocks,)),
            ],
            compiler_params=pltpu.CompilerParams(
                collective_id=0, has_side_effects=True, vmem_limit_bytes=VMEM_BYTES
            ),
        )(
            pltpu.with_memory_space_constraint(momentum, pltpu.HBM),
            pltpu.with_memory_space_constraint(gradient, pltpu.HBM),
            pltpu.with_memory_space_constraint(columns.reshape(1, rank), pltpu.HBM),
        )
        return pl.pallas_call(
            functools.partial(finish_kernel, replicas, blocks),
            out_shape=(
                jax.ShapeDtypeStruct((rows, cols // replicas), jnp.bfloat16),
                jax.ShapeDtypeStruct((1, rows, cols), jnp.float32),
            ),
            in_specs=[vmem_space, vmem_space, vmem_space],
            out_specs=(vmem_space, hbm_space),
            scratch_shapes=[pltpu.VMEM((rows, cols), jnp.float32), dma((2 * ITERS,))],
            compiler_params=pltpu.CompilerParams(vmem_limit_bytes=VMEM_BYTES),
        )(full, current, basis)

    return jax.shard_map(
        body,
        mesh=mesh,
        in_specs=(P("dp", "mp", None), P("dp", "mp", None), P()),
        out_specs=(P("mp", "dp"), P("dp", "mp", None)),
        check_vma=False,
    )
```

```python
import functools
import math

import jax
import jax.numpy as jnp
from jax import lax
from jax.experimental import pallas as pl
from jax.experimental.pallas import tpu as pltpu
from jax.sharding import PartitionSpec as P

ITERS = 5
BLOCK = 64
CHUNK_BLOCKS = 80

inertia = 0.9
linear_term = 3.4445
cubic_term = -4.775
quintic_term = 2.0315
VMEM_BYTES = 24 * 2**20
MESH = pl.DeviceIdType.MESH


def cos_sin(index, period):
    quarter = period // 4
    turns = jnp.floor(index * (1.0 / quarter) + 0.5)
    angle = (index - turns * quarter) * (2.0 * math.pi / period)
    quadrant = turns - 4.0 * jnp.floor(turns * 0.25)
    x2 = angle * angle
    sine = angle * (
        1.0 + x2 * (-1.0 / 6 + x2 * (1.0 / 120 + x2 * (-1.0 / 5040 + x2 * (1.0 / 362880))))
    )
    cosine = 1.0 + x2 * (
        -0.5 + x2 * (1.0 / 24 + x2 * (-1.0 / 720 + x2 * (1.0 / 40320 - x2 * (1.0 / 3628800))))
    )
    odd = (quadrant == 1.0) | (quadrant == 3.0)
    cos_part = jnp.where(odd, sine, cosine)
    sin_part = jnp.where(odd, cosine, sine)
    cos_out = jnp.where((quadrant == 1.0) | (quadrant == 2.0), -cos_part, cos_part)
    sin_out = jnp.where(quadrant >= 2.0, -sin_part, sin_part)
    return cos_out, sin_out


def split(x):
    high = x.astype(jnp.bfloat16)
    return high, (x - high.astype(jnp.float32)).astype(jnp.bfloat16)


def dot(a, b, dims=((1,), (0,))):
    return lax.dot_general(a, b, (dims, ((), ())), preferred_element_type=jnp.float32)


def dot3(a, b, dims=((1,), (0,))):
    (i,), (j,) = dims
    return dot(
        jnp.concatenate([a[0], a[0], a[1]], axis=i), jnp.concatenate([b[0], b[1], b[0]], axis=j), dims
    )


def kernel(
    replicas,
    blocks,
    momentum_hbm,
    gradient_hbm,
    columns_hbm,
    full_out,
    current,
    basis,
    columns_ref,
    grad,
    cos_high,
    sin_high,
    encoded,
    swap_in,
    parts,
    full,
    columns_sem,
    load_sems,
    swap_sems,
    z_send,
    z_recv,
    m_send,
    m_recv,
    f_send,
    f_recv,
):
    rows, cols = current.shape
    rank = basis.shape[1]
    half = rows // 2
    pairs = replicas // 2
    chunk = BLOCK * CHUNK_BLOCKS
    chunks = cols // chunk
    me_dp = lax.axis_index("dp")
    me_mp = lax.axis_index("mp")
    core = lax.rem(me_dp, 2)
    me_z = lax.div(me_dp, 2)
    partner = me_dp + 1 - 2 * core

    def load(step):
        span = pl.ds(pl.multiple_of(step * chunk, chunk), chunk)
        return (
            pltpu.make_async_copy(
                momentum_hbm.at[0, :, span], current.at[:, span], load_sems.at[0, step]
            ),
            pltpu.make_async_copy(
                gradient_hbm.at[0, :, span], grad.at[:, span], load_sems.at[1, step]
            ),
        )

    columns_copy = pltpu.make_async_copy(columns_hbm, columns_ref, columns_sem)
    columns_copy.start()
    for step in range(chunks):
        for copy in load(step):
            copy.start()

    def z_peer(offset):
        return lax.rem(me_z + offset, pairs)

    def m_peer(offset):
        return lax.rem(me_mp + offset, blocks)

    barrier = pltpu.get_barrier_semaphore()
    pl.semaphore_signal(
        barrier, inc=1, device_id={"dp": partner, "mp": me_mp}, device_id_type=MESH
    )
    for offset in range(1, pairs):
        pl.semaphore_signal(
            barrier,
            inc=1,
            device_id={"dp": 2 * z_peer(offset) + core, "mp": me_mp},
            device_id_type=MESH,
        )
    for offset in range(1, blocks):
        pl.semaphore_signal(
            barrier,
            inc=1,
            device_id={"dp": me_dp, "mp": m_peer(offset)},
            device_id_type=MESH,
        )

    columns_copy.wait()
    frequency = columns_ref[...].astype(jnp.float32)
    scale = jnp.where(columns_ref[...] == 0, math.sqrt(1.0 / cols), math.sqrt(2.0 / cols))
    high_count = cos_high.shape[0]
    high_index = lax.broadcasted_iota(jnp.int32, (high_count, rank), 0).astype(jnp.float32)
    ch, sh = cos_sin(high_index * frequency, 2 * cols // BLOCK)
    cos_high[...] = ch
    sin_high[...] = sh
    low_index = lax.broadcasted_iota(jnp.int32, (BLOCK, rank), 0).astype(jnp.float32)
    cl, sl = cos_sin((2.0 * low_index + 1.0) * frequency, 4 * cols)
    cl = cl * scale
    sl = sl * scale

    encoded[...] = jnp.zeros_like(encoded)

    def encode(step, carry):
        for block in range(CHUNK_BLOCKS):
            index = step * CHUNK_BLOCKS + block
            table = cos_high[pl.ds(index, 1), :] * cl - sin_high[pl.ds(index, 1), :] * sl
            start = pl.multiple_of(index * BLOCK, BLOCK)
            basis[pl.ds(start, BLOCK), :] = table.astype(jnp.bfloat16)
        for copy in load(step):
            copy.wait()
        span = pl.ds(pl.multiple_of(step * chunk, chunk), chunk)
        now = inertia * current[:, span] + grad[:, span].astype(jnp.float32)
        current[:, span] = now
        encoded[...] += dot(now.astype(jnp.bfloat16), basis[span, :])
        return carry

    lax.fori_loop(0, chunks, encode, 0)

    pl.semaphore_wait(barrier, 1 + (pairs - 1) + (blocks - 1))

    mine = pl.ds(pl.multiple_of(core * half, half), half)
    theirs = pl.ds(pl.multiple_of((1 - core) * half, half), half)
    swap = pltpu.make_async_remote_copy(
        src_ref=encoded.at[theirs, :],
        dst_ref=swap_in,
        send_sem=swap_sems.at[0],
        recv_sem=swap_sems.at[1],
        device_id={"dp": partner, "mp": me_mp},
        device_id_type=MESH,
    )
    swap.start()
    swap.wait()
    parts[me_z] = encoded[mine, :] + swap_in[...]

    z_copies = []
    for offset in range(1, pairs):
        copy = pltpu.make_async_remote_copy(
            src_ref=parts.at[me_z],
            dst_ref=parts.at[me_z],
            send_sem=z_send.at[offset],
            recv_sem=z_recv.at[offset],
            device_id={"dp": 2 * z_peer(offset) + core, "mp": me_mp},
            device_id_type=MESH,
        )
        copy.start()
        z_copies.append(copy)
    for copy in z_copies:
        copy.wait()
    total = parts[0]
    for index in range(1, pairs):
        total = total + parts[index]
    full[me_mp, core] = total * (1.0 / replicas)

    def forward(index):
        return pltpu.make_async_remote_copy(
            src_ref=full.at[index, core],
            dst_ref=full.at[index, core],
            send_sem=f_send.at[index],
            recv_sem=f_recv.at[index],
            device_id={"dp": partner, "mp": me_mp},
            device_id_type=MESH,
        )

    m_copies = []
    for offset in range(1, blocks):
        copy = pltpu.make_async_remote_copy(
            src_ref=full.at[me_mp, core],
            dst_ref=full.at[me_mp, core],
            send_sem=m_send.at[offset],
            recv_sem=m_recv.at[offset],
            device_id={"dp": me_dp, "mp": m_peer(offset)},
            device_id_type=MESH,
        )
        copy.start()
        m_copies.append(copy)
    own = forward(me_mp)
    own.start()
    own.wait()

    passed = []
    for offset in range(1, blocks):
        m_copies[offset - 1].wait()
        copy = forward(lax.rem(me_mp + blocks - offset, blocks))
        copy.start()
        passed.append(copy)
    for copy in passed:
        copy.wait()

    full_out[...] = full[...].reshape(full_out.shape)


def finish_kernel(
    replicas, blocks, full_ref, current, basis, update_ref, new_hbm, out, store_sems
):
    rows, cols = current.shape
    rank = basis.shape[1]
    chunk = cols // (2 * ITERS)
    me_dp = lax.axis_index("dp")
    me_mp = lax.axis_index("mp")

    own_rows = full_ref[pl.ds(pl.multiple_of(me_mp * rows, rows), rows), :]
    coded = own_rows.astype(jnp.bfloat16)

    def store(step):
        span = pl.ds(step * chunk, chunk)
        return pltpu.make_async_copy(
            out.at[:, span], new_hbm.at[0, :, span], store_sems.at[step]
        )

    def refresh(step):
        span = pl.ds(step * chunk, chunk)
        out[:, span] = current[:, span] - dot(coded, basis[span, :], ((1,), (1,)))

    for step in range(2 * ITERS):
        refresh(step)
        store(step).start()
    averaged = full_ref[...]
    pair = split(averaged)
    gram = dot3(pair, pair, ((0,), (0,)))
    inverse = lax.rsqrt(jnp.full((1, 1), 1e-06, jnp.float32) + jnp.sum(averaged * averaged))
    g = gram * (inverse * inverse)
    x = own_rows * inverse
    row = lax.broadcasted_iota(jnp.int32, (rank, rank), 0)
    col = lax.broadcasted_iota(jnp.int32, (rank, rank), 1)
    diagonal = jnp.where(row == col, linear_term, 0.0)
    for index in range(ITERS):
        g_pair = split(g)
        p = diagonal + cubic_term * g + quintic_term * dot3(g_pair, g_pair)
        p_pair = split(p)
        x = dot3(split(x), p_pair)
        if index < ITERS - 1:
            g = dot3(p_pair, split(dot3(p_pair, g_pair)))

    band = cols // replicas
    band_basis = basis[pl.ds(pl.multiple_of(me_dp * band, 16), band), :]
    direction = dot(x.astype(jnp.bfloat16), band_basis, ((1,), (1,)))
    update_scale = math.sqrt(rows * blocks * cols / rank)
    update_ref[...] = (direction * update_scale).astype(jnp.bfloat16)
    for step in range(2 * ITERS):
        store(step).wait()


def solution(mesh):
    replicas, blocks = mesh.shape["dp"], mesh.shape["mp"]

    def body(momentum, gradient, columns):
        _, rows, cols = momentum.shape
        rank = columns.shape[0]
        chunks = cols // (BLOCK * CHUNK_BLOCKS)
        pairs = replicas // 2
        dma = pltpu.SemaphoreType.DMA
        hbm_space = pl.BlockSpec(memory_space=pltpu.HBM)
        vmem_space = pl.BlockSpec(memory_space=pltpu.VMEM)
        full, current, basis = pl.pallas_call(
            functools.partial(kernel, replicas, blocks),
            out_shape=(
                jax.ShapeDtypeStruct((blocks * rows, rank), jnp.float32),
                jax.ShapeDtypeStruct((rows, cols), jnp.float32),
                jax.ShapeDtypeStruct((cols, rank), jnp.bfloat16),
            ),
            in_specs=[hbm_space, hbm_space, hbm_space],
            out_specs=(vmem_space, vmem_space, vmem_space),
            scratch_shapes=[
                pltpu.VMEM((1, rank), jnp.int32),
                pltpu.VMEM((rows, cols), jnp.bfloat16),
                pltpu.VMEM((cols // BLOCK, rank), jnp.float32),
                pltpu.VMEM((cols // BLOCK, rank), jnp.float32),
                pltpu.VMEM((rows, rank), jnp.float32),
                pltpu.VMEM((rows // 2, rank), jnp.float32),
                pltpu.VMEM((pairs, rows // 2, rank), jnp.float32),
                pltpu.VMEM((blocks, 2, rows // 2, rank), jnp.float32),
                dma,
                dma((2, chunks)),
                dma((2,)),
                dma((pairs,)),
                dma((pairs,)),
                dma((blocks,)),
                dma((blocks,)),
                dma((blocks,)),
                dma((blocks,)),
            ],
            compiler_params=pltpu.CompilerParams(
                collective_id=0, has_side_effects=True, vmem_limit_bytes=VMEM_BYTES
            ),
        )(
            pltpu.with_memory_space_constraint(momentum, pltpu.HBM),
            pltpu.with_memory_space_constraint(gradient, pltpu.HBM),
            pltpu.with_memory_space_constraint(columns.reshape(1, rank), pltpu.HBM),
        )
        return pl.pallas_call(
            functools.partial(finish_kernel, replicas, blocks),
            out_shape=(
                jax.ShapeDtypeStruct((rows, cols // replicas), jnp.bfloat16),
                jax.ShapeDtypeStruct((1, rows, cols), jnp.float32),
            ),
            in_specs=[vmem_space, vmem_space, vmem_space],
            out_specs=(vmem_space, hbm_space),
            scratch_shapes=[pltpu.VMEM((rows, cols), jnp.float32), dma((2 * ITERS,))],
            compiler_params=pltpu.CompilerParams(vmem_limit_bytes=VMEM_BYTES),
        )(full, current, basis)

    return jax.shard_map(
        body,
        mesh=mesh,
        in_specs=(P("dp", "mp", None), P("dp", "mp", None), P()),
        out_specs=(P("mp", "dp"), P("dp", "mp", None)),
        check_vma=False,
    )
```
